32 devices in a mesh: dp: 4 (over x, core), fsdp: 8 (over z, y).
Axes of the slice: x: 2, y: 2, z: 4, core: 2. Of those that a mesh axis runs over, the one named last changes fastest.
Arguments:
- tokens: bfloat16 [4, 1024, 768], P('dp', 'fsdp'), may hold values from -6 to 6
- ln1_gain: bfloat16 [768], P('fsdp'), may hold values from 0.099609375 to 1.8984375
- ln1_bias: bfloat16 [768], P('fsdp'), may hold values from -1.75 to 1.75
- ln2_gain: bfloat16 [768], P('fsdp'), may hold values from 0.099609375 to 1.8984375
- ln2_bias: bfloat16 [768], P('fsdp'), may hold values from -1.75 to 1.75
- qkv_weight: bfloat16 [768, 2304], P('fsdp'), may hold values from -0.21875 to 0.21875
- qkv_bias: bfloat16 [2304], P('fsdp'), may hold values from -3 to 3
- out_weight: bfloat16 [768, 768], P('fsdp'), may hold values from -1.75 to 1.75
- out_bias: bfloat16 [768], P('fsdp'), may hold values from -3 to 3
- up_weight: bfloat16 [768, 3072], P('fsdp'), may hold values from -0.21875 to 0.21875
- up_bias: bfloat16 [3072], P('fsdp'), may hold values from -3 to 3
- down_weight: bfloat16 [3072, 768], P('fsdp'), may hold values from -0.109375 to 0.109375
- down_bias: bfloat16 [768], P('fsdp'), may hold values from -3 to 3
- cotangent: bfloat16 [4, 1024, 768], P('dp', 'fsdp'), may hold values from -6 to 6
Outputs:
- layer_output: bfloat16 [4, 1024, 768], P('dp', 'fsdp')
- input_grad: float32 [4, 1024, 768], P('dp', 'fsdp')
- grad_ln1_gain: float32 [768], P('fsdp')
- grad_ln1_bias: float32 [768], P('fsdp')
- grad_ln2_gain: float32 [768], P('fsdp')
- grad_ln2_bias: float32 [768], P('fsdp')
- grad_qkv_weight: float32 [768, 2304], P('fsdp')
- grad_qkv_bias: float32 [2304], P('fsdp')
- grad_out_weight: float32 [768, 768], P('fsdp')
- grad_out_bias: float32 [768], P('fsdp')
- grad_up_weight: float32 [768, 3072], P('fsdp')
- grad_up_bias: float32 [3072], P('fsdp')
- grad_down_weight: float32 [3072, 768], P('fsdp')
- grad_down_bias: float32 [768], P('fsdp')
The draws below stay inside these ranges and needn't reach their ends.
All inputs are finite; a program needn't handle non-finite values.
Results may differ from the reference program's by a relative error of at most 0.018.
Values may be sent and summed in bfloat16 or wider, within the bound.
A program may use at most 128 MiB of HBM per device.

```python
import jax
import jax.numpy as jnp
from jax import lax

D = 768
HEADS = 12
HEAD = 64
ROT = 16
FF = 3072
SEQS = 4
LEN = 1024


def shard_levels(own_key, shape, cuts, least, top_value):
    def one(axis_at, blocks):
        heights = jax.random.uniform(jax.random.fold_in(jax.random.fold_in(own_key, 6), axis_at), (blocks,), jnp.float32, least / len(cuts), top_value / len(cuts))
        return jnp.repeat(jnp.exp(heights), shape[axis_at] // blocks).reshape((-1,) + (1,) * (len(shape) - axis_at - 1))

    level = one(*cuts[0])
    for cut in cuts[1:]:
        level = level * one(*cut)
    return level


def centred(key, shape, deviation, bound, shards=(), kind=jnp.bfloat16):
    values = deviation * jax.random.normal(key, shape, jnp.float32)
    if shards:
        values = values * shard_levels(key, shape, shards, -0.22, 0.18)
    return jnp.clip(values, -bound, bound).astype(kind)


def setup_inputs(seed: int = 0) -> dict:
    arg_keys = jax.random.split(jax.random.key(seed), 15)
    return {
        "tokens": centred(arg_keys[0], (SEQS, LEN, D), 1.0, 6.0, ((0, 4), (1, 8))),
        "ln1_gain": jnp.clip(1.0 + 0.18 * jax.random.normal(arg_keys[1], (D,), jnp.float32), 0.099609375, 1.8984375).astype(jnp.bfloat16),
        "ln1_bias": centred(arg_keys[2], (D,), 0.3, 1.75, ((0, 8),)),
        "ln2_gain": jnp.clip(1.0 + 0.18 * jax.random.normal(arg_keys[3], (D,), jnp.float32), 0.099609375, 1.8984375).astype(jnp.bfloat16),
        "ln2_bias": centred(arg_keys[4], (D,), 0.3, 1.75, ((0, 8),)),
        "qkv_weight": centred(arg_keys[5], (D, 3 * D), D ** -0.5, 0.21875, ((0, 8),)),
        "qkv_bias": centred(arg_keys[6], (3 * D,), 0.5, 3.0, ((0, 8),)),
        "out_weight": centred(arg_keys[7], (D, D), (max(1, D // 64)) ** -0.5, 1.75, ((0, 8),)),
        "out_bias": centred(arg_keys[8], (D,), 0.5, 3.0, ((0, 8),)),
        "up_weight": centred(arg_keys[9], (D, FF), D ** -0.5, 0.21875, ((0, 8),)),
        "up_bias": centred(arg_keys[10], (FF,), 0.5, 3.0, ((0, 8),)),
        "down_weight": centred(arg_keys[11], (FF, D), FF ** -0.5, 0.109375, ((0, 8),)),
        "down_bias": centred(arg_keys[12], (D,), 0.5, 3.0, ((0, 8),)),
        "cotangent": centred(arg_keys[13], (SEQS, LEN, D), 1.0, 6.0, ((0, 4), (1, 8))),
    }


@jax.custom_vjp
def low(v):
    return lax.optimization_barrier(v.astype(jnp.bfloat16)).astype(jnp.float32)

@jax.custom_vjp
def low_back(v):
    return v

def low_keep(v):
    return (low(v), None)

def low_pass(kept, grad):
    return (grad,)

def back_keep(v):
    return (v, None)

def back_low(kept, grad):
    return (low(grad),)
low.defvjp(low_keep, low_pass)
low_back.defvjp(back_keep, back_low)
highest = lax.Precision.HIGHEST

def product(left, right):
    return jnp.dot(left, right, precision=highest)

def norm_layer(inputs, gain, shift):
    center = inputs - lax.optimization_barrier(jnp.mean(inputs, axis=-1, keepdims=True))
    spread = lax.optimization_barrier(jnp.mean(center * center, axis=-1, keepdims=True))
    return center * lax.rsqrt(spread + 1e-05) * gain + shift

def rotate(tensor, places):
    half = ROT // 2
    inverse = 10000.0 ** (-(jnp.arange(half, dtype=jnp.float32) * 2.0) / ROT)
    angle = places[:, None] * inverse[None, :]
    cosine = jnp.cos(angle)[:, None, :]
    sine = jnp.sin(angle)[:, None, :]
    first = tensor[..., :half]
    second = tensor[..., half:ROT]
    return jnp.concatenate([first * cosine - second * sine, second * cosine + first * sine, tensor[..., ROT:]], axis=-1)

def layer_fwd(inputs, gain_first, bias_first, gain_second, bias_second, w_qkv, b_qkv, w_out, b_out, w_up, b_up, w_down, b_down):
    length = inputs.shape[0]
    first_norm = low(norm_layer(inputs, gain_first, bias_first))
    second_norm = low(norm_layer(inputs, gain_second, bias_second))
    projected = low_back(product(first_norm, w_qkv) + b_qkv)
    places = jnp.arange(length, dtype=jnp.float32)
    queries = low(rotate(projected[:, :D].reshape(length, HEADS, HEAD), places) * 0.125)
    keys_all = low(rotate(projected[:, D:2 * D].reshape(length, HEADS, HEAD), places))
    values_all = low(projected[:, 2 * D:].reshape(length, HEADS, HEAD))
    query_rows = min(512, length)
    count = length // query_rows

    def attend_rows(pieces):
        query_block, start = pieces
        scores = jnp.einsum('qhd,khd->hqk', query_block, keys_all, precision=highest)
        scores = low_back(scores)
        query_places = start + jnp.arange(query_rows, dtype=jnp.int32)
        key_places = jnp.arange(length, dtype=jnp.int32)
        visible = key_places[None, :] <= query_places[:, None]
        scores = jnp.where(visible[None], scores, -1e+30)
        probs = jax.nn.softmax(scores, axis=-1)
        return jnp.einsum('hqk,khd->qhd', low(probs), values_all, precision=highest)
    starts = jnp.arange(count, dtype=jnp.int32) * query_rows
    attended = lax.map(jax.checkpoint(attend_rows), (queries.reshape(count, query_rows, HEADS, HEAD), starts))
    attended = low(low_back(attended.reshape(length, D)))
    branch_attn = product(attended, w_out) + b_out
    hidden_pre = low_back(product(second_norm, w_up) + b_up)
    hidden = low(jax.nn.gelu(hidden_pre, approximate=False))
    branch_mlp = product(hidden, w_down) + b_down
    return inputs + branch_attn + branch_mlp

def reference(tokens, ln1_gain, ln1_bias, ln2_gain, ln2_bias, qkv_weight, qkv_bias, out_weight, out_bias, up_weight, up_bias, down_weight, down_bias, cotangent):
    params = tuple((member.astype(jnp.float32) for member in (ln1_gain, ln1_bias, ln2_gain, ln2_bias, qkv_weight, qkv_bias, out_weight, out_bias, up_weight, up_bias, down_weight, down_bias)))

    def one_sequence(totals, pieces):
        seq_tokens, seq_grad = pieces
        result, pullback = jax.vjp(layer_fwd, seq_tokens.astype(jnp.float32), *params)
        grads = pullback(seq_grad.astype(jnp.float32))
        totals = tuple((summed + addend for summed, addend in zip(totals, grads[1:])))
        return (totals, (result.astype(jnp.bfloat16), grads[0]))
    initial = tuple((jnp.zeros(member.shape, jnp.float32) for member in params))
    totals, (outputs, input_grads) = lax.scan(one_sequence, initial, (tokens, cotangent))
    return (outputs, input_grads, totals[0], totals[1], totals[2], totals[3], totals[4], totals[5], totals[6], totals[7], totals[8], totals[9], totals[10], totals[11])
```

```python
import math

import jax
import jax.numpy as jnp
from jax import lax
from jax.sharding import PartitionSpec as P

HEADS = 12
HEAD = 64
ROT = 16

epsilon = 1e-05
inv_root_two = 1.0 / math.sqrt(2.0)
inv_root_twopi = 1.0 / math.sqrt(2.0 * math.pi)
bf16 = jnp.bfloat16
f32 = jnp.float32


def rotary(tensor, cosine, sine, direction):
    half = ROT // 2
    first = tensor[..., :half]
    second = tensor[..., half:ROT]
    return jnp.concatenate(
        [
            first * cosine - direction * second * sine,
            second * cosine + direction * first * sine,
            tensor[..., ROT:],
        ],
        axis=-1,
    )


def dot(a, b, dims):
    return lax.dot_general(a, b, ((dims[0], dims[1]), ((), ())), preferred_element_type=f32)


NN = ((1,), (0,))
NT = ((1,), (1,))
TN = ((0,), (0,))


def gather_rows(arrays):
    return [lax.all_gather(a, "fsdp", axis=0, tiled=True) for a in arrays]


def scatter_rows(a):
    return lax.psum_scatter(a, "fsdp", scatter_dimension=0, tiled=True)


def spread_weights(blocks):
    return lax.all_to_all(blocks, "fsdp", 0, 0, tiled=True)


def return_grads(blocks, own):
    summed = lax.psum(blocks, "dp")
    own = lax.psum(own, "dp")
    return lax.all_to_all(summed, "fsdp", 0, 0, tiled=True), own


def body(
    tokens,
    ln1_gain,
    ln1_bias,
    ln2_gain,
    ln2_bias,
    qkv_weight,
    qkv_bias,
    out_weight,
    out_bias,
    up_weight,
    up_bias,
    down_weight,
    down_bias,
    cotangent,
):
    rank = lax.axis_index("fsdp")
    F = lax.axis_size("fsdp")
    rows, D = tokens.shape[1:]
    W = D // F
    FFW = down_weight.shape[0]
    NH = max(-(-((g * W) % HEAD + W) // HEAD) for g in range(F))
    WIN = NH * HEAD
    starts = [min(g * W // HEAD, HEADS - NH) * HEAD for g in range(F)]
    start = jnp.minimum(rank * W // HEAD, HEADS - NH) * HEAD
    off = rank * W - start
    S = rows * F

    qkv3 = qkv_weight.reshape(W, 3, D)
    blocks = jnp.stack(
        [
            jnp.concatenate(
                [
                    qkv3[:, 0, s : s + WIN],
                    qkv3[:, 1, s : s + WIN],
                    qkv3[:, 2, s : s + WIN],
                    up_weight[:, g * FFW : (g + 1) * FFW],
                ],
                axis=1,
            )
            for g, s in enumerate(starts)
        ]
    )
    smalls = jnp.concatenate(
        [ln1_gain, ln1_bias, ln2_gain, ln2_bias, out_bias, down_bias, qkv_bias]
    )[None]
    x_low, small_all = gather_rows([tokens[0], smalls])
    wall = spread_weights(blocks).reshape(D, 3 * WIN + FFW)
    w_qkv = wall[:, : 3 * WIN]
    w_up = wall[:, 3 * WIN :]
    up_ring = [(i, (i + 1) % F) for i in range(F)]
    down_ring = [(i, (i - 1) % F) for i in range(F)]
    out_prev = lax.ppermute(out_weight, "fsdp", up_ring)
    out_next = lax.ppermute(out_weight, "fsdp", down_ring)
    (grad_out,) = gather_rows([cotangent[0]])
    out_three = jnp.concatenate(
        [out_prev, out_weight, out_next, jnp.zeros((WIN, D), bf16)], axis=0
    )
    w_out_win = lax.dynamic_slice_in_dim(out_three, W - off, WIN, 0)
    win_col = jnp.arange(WIN, dtype=jnp.int32)
    mine = (win_col >= off) & (win_col < off + W)
    small_all = small_all.astype(f32)
    gain_one, bias_one, gain_two, bias_two, b_out, b_down = [
        small_all[:, i * W : (i + 1) * W].reshape(D) for i in range(6)
    ]
    b_qkv = small_all[:, 6 * W :].reshape(3, D)
    b_qkv = lax.dynamic_slice_in_dim(b_qkv, start, WIN, 1).reshape(3 * WIN)
    b_up = up_bias.astype(f32)

    x = x_low.astype(f32)
    center = x - jnp.mean(x, axis=-1, keepdims=True)
    inverse = lax.rsqrt(jnp.mean(center * center, axis=-1, keepdims=True) + epsilon)
    normed = center * inverse
    first_low = (normed * gain_one + bias_one).astype(bf16)
    second_low = (normed * gain_two + bias_two).astype(bf16)

    places = jnp.arange(S, dtype=f32)
    half = ROT // 2
    freq = 10000.0 ** (-(jnp.arange(half, dtype=f32) * 2.0) / ROT)
    angle = places[:, None] * freq[None, :]
    cosine = jnp.cos(angle)[:, None, :]
    sine = jnp.sin(angle)[:, None, :]

    proj = dot(first_low, w_qkv, NN) + b_qkv
    queries = (rotary(proj[:, :WIN].reshape(S, NH, HEAD), cosine, sine, 1.0) * 0.125).astype(bf16)
    keys = rotary(proj[:, WIN : 2 * WIN].reshape(S, NH, HEAD), cosine, sine, 1.0).astype(bf16)
    vals = proj[:, 2 * WIN :].astype(bf16).reshape(S, NH, HEAD)
    q_place = jnp.arange(S, dtype=jnp.int32)
    visible = (q_place[None, :] <= q_place[:, None])[None]
    scores = jnp.einsum("qhd,khd->hqk", queries, keys, preferred_element_type=f32)
    masked = jnp.where(visible, scores, -1e30)
    top = jnp.max(masked, axis=-1, keepdims=True)
    lse = top + jnp.log(jnp.sum(jnp.exp(masked - top), axis=-1, keepdims=True))
    probs = jnp.exp(masked - lse)
    probs_low = probs.astype(bf16)
    attended = jnp.einsum("hqk,khd->qhd", probs_low, vals, preferred_element_type=f32)
    att_low = jnp.where(mine, attended.reshape(S, WIN), 0.0).astype(bf16)

    hidden_pre = dot(second_low, w_up, NN) + b_up
    cdf = 0.5 * (1.0 + lax.erf(hidden_pre * inv_root_two))
    hidden_low = (hidden_pre * cdf).astype(bf16)
    part = dot(att_low, w_out_win, NN) + dot(hidden_low, down_weight, NN)
    branch = scatter_rows(part.astype(bf16)).astype(f32)

    grad_hidden = dot(grad_out, down_weight, NT)
    slope = cdf + hidden_pre * jnp.exp(-0.5 * hidden_pre * hidden_pre) * inv_root_twopi
    grad_pre = (grad_hidden * slope).astype(bf16)
    grad_w_down = dot(hidden_low, grad_out, TN)
    grad_w_out_win = dot(att_low, grad_out, TN)
    grad_w_out = lax.dynamic_slice_in_dim(grad_w_out_win, off, W, 0)
    bias_total = jnp.sum(grad_out.astype(f32), axis=0)
    grad_b_up = jnp.sum(grad_pre.astype(f32), axis=0)
    grad_att = dot(grad_out, w_out_win, NT).astype(bf16).reshape(S, NH, HEAD)
    delta = jnp.transpose(jnp.sum(grad_att.astype(f32) * attended, axis=-1))[:, :, None]
    grad_probs = jnp.einsum("qhd,khd->hqk", grad_att, vals, preferred_element_type=f32)
    grad_scores = (probs * (grad_probs - delta)).astype(bf16)
    grad_q = jnp.einsum("hqk,khd->qhd", grad_scores, keys, preferred_element_type=f32)
    grad_k = jnp.einsum("hqk,qhd->khd", grad_scores, queries, preferred_element_type=f32)
    grad_v = jnp.einsum("hqk,qhd->khd", probs_low, grad_att, preferred_element_type=f32)
    grad_proj = jnp.stack(
        [
            rotary(grad_q * 0.125, cosine, sine, -1.0).reshape(S, WIN),
            rotary(grad_k, cosine, sine, -1.0).reshape(S, WIN),
            grad_v.reshape(S, WIN),
        ],
        axis=1,
    )
    grad_proj = jnp.where(mine, grad_proj, 0.0).astype(bf16).reshape(S, 3 * WIN)
    grad_w_qkv = dot(first_low, grad_proj, TN)
    grad_w_up = dot(second_low, grad_pre, TN)
    grad_b_qkv = jnp.sum(grad_proj.astype(f32), axis=0).reshape(3, WIN)
    grad_first = dot(grad_proj, w_qkv, NT)
    grad_second = dot(grad_pre, w_up, NT)
    vectors = [
        jnp.sum(grad_first * normed, axis=0),
        jnp.sum(grad_first, axis=0),
        jnp.sum(grad_second * normed, axis=0),
        jnp.sum(grad_second, axis=0),
    ]
    mixed = grad_first * gain_one + grad_second * gain_two
    b_full = lax.dynamic_update_slice_in_dim(jnp.zeros((3, D), f32), grad_b_qkv, start, 1)
    small_part = jnp.concatenate(
        [v.reshape(F, W) for v in vectors] + [b_full.reshape(F, 3 * W)], axis=1
    )
    mixed_mine = scatter_rows(mixed.astype(bf16)).astype(f32)
    small_mine = scatter_rows(small_part)[0]
    own_small = jnp.concatenate(
        [small_mine, lax.dynamic_slice_in_dim(bias_total, rank * W, W, 0), grad_b_up]
    )
    own_small = lax.psum(own_small, "dp")

    grad_blocks = jnp.concatenate([grad_w_qkv, grad_w_up], axis=1).astype(bf16)
    grad_blocks = grad_blocks.reshape(F, W, 3 * WIN + FFW)
    own = jnp.concatenate([grad_w_out, grad_w_down], axis=0).astype(bf16)
    returned, own = return_grads(grad_blocks, own)
    returned = returned.astype(f32)
    own = own.astype(f32)
    pieces = [
        [returned[g, :, i * WIN + g * W - s : i * WIN + g * W - s + W] for g, s in enumerate(starts)]
        for i in range(3)
    ]
    out_w_qkv = jnp.concatenate(pieces[0] + pieces[1] + pieces[2], axis=1)
    out_w_up = jnp.concatenate([returned[g, :, 3 * WIN :] for g in range(F)], axis=1)

    here = rank * rows
    x_own = tokens[0].astype(f32)
    c_own = x_own - jnp.mean(x_own, axis=-1, keepdims=True)
    i_own = lax.rsqrt(jnp.mean(c_own * c_own, axis=-1, keepdims=True) + epsilon)
    n_own = c_own * i_own
    layer_output = (x_own + branch + b_out + b_down).astype(bf16)
    input_grad = cotangent[0].astype(f32) + i_own * (
        mixed_mine
        - jnp.mean(mixed_mine, axis=-1, keepdims=True)
        - n_own * jnp.mean(mixed_mine * n_own, axis=-1, keepdims=True)
    )
    g = [own_small[i * W : (i + 1) * W] for i in range(4)]
    bias_mine = own_small[7 * W : 8 * W]
    return (
        layer_output[None],
        input_grad[None],
        g[0],
        g[1],
        g[2],
        g[3],
        out_w_qkv,
        own_small[4 * W : 7 * W],
        own[:W],
        bias_mine,
        out_w_up,
        own_small[8 * W :],
        own[W:],
        bias_mine,
    )


def solution(mesh):
    row = P("fsdp", None)
    vec = P("fsdp")
    act = P("dp", "fsdp", None)
    return jax.shard_map(
        body,
        mesh=mesh,
        in_specs=(act, vec, vec, vec, vec, row, vec, row, vec, row, vec, row, vec, act),
        out_specs=(act, act, vec, vec, vec, vec, row, vec, row, vec, row, vec, row, vec),
        check_vma=False,
    )
```

```python
import math

import jax
import jax.numpy as jnp
from jax import lax
from jax.sharding import PartitionSpec as P

HEADS = 12
HEAD = 64
ROT = 16

epsilon = 1e-05
inv_root_two = 1.0 / math.sqrt(2.0)
inv_root_twopi = 1.0 / math.sqrt(2.0 * math.pi)
bf16 = jnp.bfloat16
f32 = jnp.float32


def rotary(tensor, cosine, sine, direction):
    half = ROT // 2
    first = tensor[..., :half]
    second = tensor[..., half:ROT]
    return jnp.concatenate(
        [
            first * cosine - direction * second * sine,
            second * cosine + direction * first * sine,
            tensor[..., ROT:],
        ],
        axis=-1,
    )


def dot(a, b, dims):
    return lax.dot_general(a, b, ((dims[0], dims[1]), ((), ())), preferred_element_type=f32)


NN = ((1,), (0,))
NT = ((1,), (1,))
TN = ((0,), (0,))


def gather_rows(arrays):
    return [lax.all_gather(a, "fsdp", axis=0, tiled=True) for a in arrays]


def scatter_rows(a):
    F = lax.axis_size("fsdp")
    got = lax.all_to_all(a, "fsdp", 0, 0, tiled=True)
    return jnp.sum(got.reshape((F, a.shape[0] // F) + a.shape[1:]).astype(f32), axis=0)


def spread_weights(blocks):
    return lax.all_to_all(blocks, "fsdp", 0, 0, tiled=True)


def return_grads(blocks, own):
    n = lax.axis_size("dp")
    F, W, C = blocks.shape
    R, D = own.shape
    parts = jnp.swapaxes(blocks.reshape(F, n, W // n, C), 0, 1).reshape(n, F * (W // n), C)
    own_parts = own.reshape(n, R // n, D)
    if C == D:
        both = jnp.concatenate([parts, own_parts], axis=1)
        both = jnp.sum(lax.all_to_all(both, "dp", 0, 0, tiled=True).astype(f32), axis=0)
        part, own_part = both[: F * (W // n)].astype(bf16), both[F * (W // n) :].astype(bf16)
    else:
        part = jnp.sum(lax.all_to_all(parts, "dp", 0, 0, tiled=True).astype(f32), axis=0)
        own_part = jnp.sum(lax.all_to_all(own_parts, "dp", 0, 0, tiled=True).astype(f32), axis=0)
        part, own_part = part.astype(bf16), own_part.astype(bf16)
    part = lax.all_to_all(part, "fsdp", 0, 0, tiled=True)
    if C == D:
        whole = lax.all_gather(jnp.concatenate([part, own_part], axis=0), "dp", axis=0)
        part_all, own_all = whole[:, : F * (W // n)], whole[:, F * (W // n) :]
    else:
        part_all = lax.all_gather(part, "dp", axis=0)
        own_all = lax.all_gather(own_part, "dp", axis=0)
    part_all = jnp.swapaxes(part_all.reshape(n, F, W // n, C), 0, 1).reshape(F, W, C)
    return part_all, own_all.reshape(R, D)


def body(
    tokens,
    ln1_gain,
    ln1_bias,
    ln2_gain,
    ln2_bias,
    qkv_weight,
    qkv_bias,
    out_weight,
    out_bias,
    up_weight,
    up_bias,
    down_weight,
    down_bias,
    cotangent,
):
    rank = lax.axis_index("fsdp")
    F = lax.axis_size("fsdp")
    rows, D = tokens.shape[1:]
    W = D // F
    FFW = down_weight.shape[0]
    NH = max(-(-((g * W) % HEAD + W) // HEAD) for g in range(F))
    WIN = NH * HEAD
    starts = [min(g * W // HEAD, HEADS - NH) * HEAD for g in range(F)]
    start = jnp.minimum(rank * W // HEAD, HEADS - NH) * HEAD
    off = rank * W - start
    S = rows * F

    qkv3 = qkv_weight.reshape(W, 3, D)
    blocks = jnp.stack(
        [
            jnp.concatenate(
                [
                    qkv3[:, 0, s : s + WIN],
                    qkv3[:, 1, s : s + WIN],
                    qkv3[:, 2, s : s + WIN],
                    up_weight[:, g * FFW : (g + 1) * FFW],
                ],
                axis=1,
            )
            for g, s in enumerate(starts)
        ]
    )
    smalls = jnp.concatenate(
        [ln1_gain, ln1_bias, ln2_gain, ln2_bias, out_bias, down_bias, qkv_bias]
    )
    extra = -(-smalls.shape[0] // (16 * D)) * 16
    smalls = jnp.concatenate([smalls, jnp.zeros(extra * D - smalls.shape[0], bf16)])
    (both_all,) = gather_rows([jnp.concatenate([tokens[0], smalls.reshape(extra, D)], axis=0)])
    both_all = both_all.reshape(F, rows + extra, D)
    x_low = both_all[:, :rows].reshape(S, D)
    small_all = both_all[:, rows:].reshape(F, extra * D)
    wall = spread_weights(blocks).reshape(D, 3 * WIN + FFW)
    w_qkv = wall[:, : 3 * WIN]
    w_up = wall[:, 3 * WIN :]
    up_ring = [(i, (i + 1) % F) for i in range(F)]
    down_ring = [(i, (i - 1) % F) for i in range(F)]
    out_prev = lax.ppermute(out_weight, "fsdp", up_ring)
    out_next = lax.ppermute(out_weight, "fsdp", down_ring)
    (grad_out,) = gather_rows([cotangent[0]])
    out_three = jnp.concatenate(
        [out_prev, out_weight, out_next, jnp.zeros((WIN, D), bf16)], axis=0
    )
    w_out_win = lax.dynamic_slice_in_dim(out_three, W - off, WIN, 0)
    win_col = jnp.arange(WIN, dtype=jnp.int32)
    mine = (win_col >= off) & (win_col < off + W)
    small_all = small_all.astype(f32)
    gain_one, bias_one, gain_two, bias_two, b_out, b_down = [
        small_all[:, i * W : (i + 1) * W].reshape(D) for i in range(6)
    ]
    b_qkv = small_all[:, 6 * W : 9 * W].reshape(3, D)
    b_qkv = lax.dynamic_slice_in_dim(b_qkv, start, WIN, 1).reshape(3 * WIN)
    b_up = up_bias.astype(f32)

    x = x_low.astype(f32)
    center = x - jnp.mean(x, axis=-1, keepdims=True)
    inverse = lax.rsqrt(jnp.mean(center * center, axis=-1, keepdims=True) + epsilon)
    normed = center * inverse
    first_low = (normed * gain_one + bias_one).astype(bf16)
    second_low = (normed * gain_two + bias_two).astype(bf16)

    places = jnp.arange(S, dtype=f32)
    half = ROT // 2
    freq = 10000.0 ** (-(jnp.arange(half, dtype=f32) * 2.0) / ROT)
    angle = places[:, None] * freq[None, :]
    cosine = jnp.cos(angle)[:, None, :]
    sine = jnp.sin(angle)[:, None, :]

    proj = dot(first_low, w_qkv, NN) + b_qkv
    queries = (rotary(proj[:, :WIN].reshape(S, NH, HEAD), cosine, sine, 1.0) * 0.125).astype(bf16)
    keys = rotary(proj[:, WIN : 2 * WIN].reshape(S, NH, HEAD), cosine, sine, 1.0).astype(bf16)
    vals = proj[:, 2 * WIN :].astype(bf16).reshape(S, NH, HEAD)
    q_place = jnp.arange(S, dtype=jnp.int32)
    visible = (q_place[None, :] <= q_place[:, None])[None]
    scores = jnp.einsum("qhd,khd->hqk", queries, keys, preferred_element_type=f32)
    masked = jnp.where(visible, scores, -1e30)
    top = jnp.max(masked, axis=-1, keepdims=True)
    lse = top + jnp.log(jnp.sum(jnp.exp(masked - top), axis=-1, keepdims=True))
    probs = jnp.exp(masked - lse)
    probs_low = probs.astype(bf16)
    attended = jnp.einsum("hqk,khd->qhd", probs_low, vals, preferred_element_type=f32)
    att_low = jnp.where(mine, attended.reshape(S, WIN), 0.0).astype(bf16)

    hidden_pre = dot(second_low, w_up, NN) + b_up
    cdf = 0.5 * (1.0 + lax.erf(hidden_pre * inv_root_two))
    hidden_low = (hidden_pre * cdf).astype(bf16)
    part = dot(att_low, w_out_win, NN) + dot(hidden_low, down_weight, NN)
    branch = scatter_rows(part.astype(bf16))

    grad_hidden = dot(grad_out, down_weight, NT)
    slope = cdf + hidden_pre * jnp.exp(-0.5 * hidden_pre * hidden_pre) * inv_root_twopi
    grad_pre = (grad_hidden * slope).astype(bf16)
    grad_w_down = dot(hidden_low, grad_out, TN)
    grad_w_out_win = dot(att_low, grad_out, TN)
    grad_w_out = lax.dynamic_slice_in_dim(grad_w_out_win, off, W, 0)
    bias_total = jnp.sum(grad_out.astype(f32), axis=0)
    grad_b_up = jnp.sum(grad_pre.astype(f32), axis=0)
    grad_att = dot(grad_out, w_out_win, NT).astype(bf16).reshape(S, NH, HEAD)
    delta = jnp.transpose(jnp.sum(grad_att.astype(f32) * attended, axis=-1))[:, :, None]
    grad_probs = jnp.einsum("qhd,khd->hqk", grad_att, vals, preferred_element_type=f32)
    grad_scores = (probs * (grad_probs - delta)).astype(bf16)
    grad_q = jnp.einsum("hqk,khd->qhd", grad_scores, keys, preferred_element_type=f32)
    grad_k = jnp.einsum("hqk,qhd->khd", grad_scores, queries, preferred_element_type=f32)
    grad_v = jnp.einsum("hqk,qhd->khd", probs_low, grad_att, preferred_element_type=f32)
    grad_proj = jnp.stack(
        [
            rotary(grad_q * 0.125, cosine, sine, -1.0).reshape(S, WIN),
            rotary(grad_k, cosine, sine, -1.0).reshape(S, WIN),
            grad_v.reshape(S, WIN),
        ],
        axis=1,
    )
    grad_proj = jnp.where(mine, grad_proj, 0.0).astype(bf16).reshape(S, 3 * WIN)
    grad_w_qkv = dot(first_low, grad_proj, TN)
    grad_w_up = dot(second_low, grad_pre, TN)
    grad_b_qkv = jnp.sum(grad_proj.astype(f32), axis=0).reshape(3, WIN)
    grad_first = dot(grad_proj, w_qkv, NT)
    grad_second = dot(grad_pre, w_up, NT)
    vectors = [
        jnp.sum(grad_first * normed, axis=0),
        jnp.sum(grad_first, axis=0),
        jnp.sum(grad_second * normed, axis=0),
        jnp.sum(grad_second, axis=0),
    ]
    mixed = grad_first * gain_one + grad_second * gain_two
    b_full = lax.dynamic_update_slice_in_dim(jnp.zeros((3, D), f32), grad_b_qkv, start, 1)
    small_part = jnp.concatenate(
        [v.reshape(F, W) for v in vectors] + [b_full.reshape(F, 3 * W)], axis=1
    )
    mixed_mine = scatter_rows(mixed.astype(bf16))
    small_mine = scatter_rows(small_part)[0]
    own_small = jnp.concatenate(
        [small_mine, lax.dynamic_slice_in_dim(bias_total, rank * W, W, 0), grad_b_up]
    )
    pad = 8 * lax.axis_size("dp")
    own_rows = -(-(W + FFW + -(-own_small.shape[0] // D)) // pad) * pad
    n_small = own_rows - W - FFW
    own_small = jnp.concatenate([own_small, jnp.zeros(n_small * D - own_small.shape[0], f32)])

    grad_blocks = jnp.concatenate([grad_w_qkv, grad_w_up], axis=1).astype(bf16)
    grad_blocks = grad_blocks.reshape(F, W, 3 * WIN + FFW)
    own = jnp.concatenate(
        [grad_w_out, grad_w_down, own_small.reshape(n_small, D)], axis=0
    ).astype(bf16)
    returned, own = return_grads(grad_blocks, own)
    returned = returned.astype(f32)
    own = own.astype(f32)
    own_small = own[W + FFW :].reshape(n_small * D)
    pieces = [
        [returned[g, :, i * WIN + g * W - s : i * WIN + g * W - s + W] for g, s in enumerate(starts)]
        for i in range(3)
    ]
    out_w_qkv = jnp.concatenate(pieces[0] + pieces[1] + pieces[2], axis=1)
    out_w_up = jnp.concatenate([returned[g, :, 3 * WIN :] for g in range(F)], axis=1)

    here = rank * rows
    x_own = tokens[0].astype(f32)
    c_own = x_own - jnp.mean(x_own, axis=-1, keepdims=True)
    i_own = lax.rsqrt(jnp.mean(c_own * c_own, axis=-1, keepdims=True) + epsilon)
    n_own = c_own * i_own
    layer_output = (x_own + branch + b_out + b_down).astype(bf16)
    input_grad = cotangent[0].astype(f32) + i_own * (
        mixed_mine
        - jnp.mean(mixed_mine, axis=-1, keepdims=True)
        - n_own * jnp.mean(mixed_mine * n_own, axis=-1, keepdims=True)
    )
    g = [own_small[i * W : (i + 1) * W] for i in range(4)]
    bias_mine = own_small[7 * W : 8 * W]
    return (
        layer_output[None],
        input_grad[None],
        g[0],
        g[1],
        g[2],
        g[3],
        out_w_qkv,
        own_small[4 * W : 7 * W],
        own[:W],
        bias_mine,
        out_w_up,
        own_small[8 * W : 8 * W + FFW],
        own[W : W + FFW],
        bias_mine,
    )


def solution(mesh):
    row = P("fsdp", None)
    vec = P("fsdp")
    act = P("dp", "fsdp", None)
    return jax.shard_map(
        body,
        mesh=mesh,
        in_specs=(act, vec, vec, vec, vec, row, vec, row, vec, row, vec, row, vec, act),
        out_specs=(act, act, vec, vec, vec, vec, row, vec, row, vec, row, vec, row, vec),
        check_vma=False,
    )
```
